256 devices in a mesh: blk: 32 (over x, y, core), slab: 8 (over z).
Axes of the slice: x: 4, y: 4, z: 8, core: 2. Of those that a mesh axis runs over, the one named last changes fastest.
Arguments:
- amplitudes: bfloat16 [960, 32768], P('blk', 'slab'), may hold values from -6 to 6
- ladder_ints: bfloat16 [32768, 32768], P('slab', 'blk'), may hold values from -0.03125 to 0.03125
- cycle_ints: bfloat16 [8, 64, 120, 512], P('slab', 'blk'), may hold values from -0.0625 to 0.0625
- block_dims: int32 [8, 2], replicated, may hold values from 24 to 64, as said below
Outputs:
- ladder_res: bfloat16 [960, 32768], P('slab', 'blk')
- cycle_res: bfloat16 [8, 512, 512], P('slab', 'blk')
The draws below stay inside these ranges and needn't reach their ends.
Inputs may be any that keep to these rules, and one draw needn't show every extreme that they name: `block_dims`: every block's two sizes lie within the padded size; in every draw some block's first size equals 64 and some block's second size equals 24.
All inputs are finite; a program needn't handle non-finite values.
Results may differ from the reference program's by a relative error of at most 0.0014.
Values may be sent and summed in bfloat16 or wider, within the bound.
A program may use at most 128 MiB of HBM per device.

```python
import jax
import jax.numpy as jnp
from jax import lax

NO = 120
BS = 64
JW = 8
IW = 8
NSB = 8
IJ = 960


def draw_block_dims(key, part):
    values = jax.random.randint(key, (NSB, 2), BS * 3 // 8, BS + 1)
    row_index = jnp.arange(NSB, dtype=jnp.int32)[:, None]
    column_index = jnp.arange(2, dtype=jnp.int32)[None, :]
    values = jnp.where((row_index == 0) & (column_index == 0), BS, values)
    values = jnp.where((row_index == NSB - 1) & (column_index == 1), BS * 3 // 8, values)
    return values.astype(jnp.int32)


def block_levels(own_key, shape, shards, least, largest):
    loudness = 1.0
    for dim, parts in shards:
        steps = jax.random.uniform(jax.random.fold_in(jax.random.fold_in(own_key, 6), dim), (parts,), jnp.float32, least / len(shards), largest / len(shards))
        loudness = loudness * jnp.repeat(jnp.exp(steps), shape[dim] // parts).reshape((-1,) + (1,) * (len(shape) - 1 - dim))
    return loudness


def scatter_about(rng, extent, scale, most, pieces=(), kind=jnp.bfloat16):
    values = scale * jax.random.normal(rng, extent, jnp.float32)
    if pieces:
        values = values * block_levels(rng, extent, pieces, -0.22, 0.18)
    return jnp.clip(values, -most, most).astype(kind)


def setup_inputs(seed: int = 0) -> dict:
    keys = jax.random.split(jax.random.key(seed), 5)
    amplitudes = scatter_about(keys[0], (IJ, NSB * BS * BS), 1.0, 6.0, ((0, 32), (1, 8)))
    ladder_ints = scatter_about(keys[1], (NSB * BS * BS, NSB * BS * BS), (NSB * BS * BS) ** -0.5, 0.03125, ((0, 8), (1, 32)))
    cycle_ints = scatter_about(keys[2], (NSB, BS, NO, IW * BS), (NO * BS) ** -0.5, 0.0625, ((0, 8), (1, 32)))
    block_dims = draw_block_dims(jax.random.fold_in(keys[4], 71), 0)
    return {"amplitudes": amplitudes, "ladder_ints": ladder_ints, "cycle_ints": cycle_ints, "block_dims": block_dims}


def column_valid(block_dims):
    column = jnp.arange(NSB * BS * BS, dtype=jnp.int32)
    owner = column // (BS * BS)
    first_index = (column // BS) % BS
    second_index = column % BS
    return (first_index < block_dims[owner, 0]) & (second_index < block_dims[owner, 1])


def reference(amplitudes, ladder_ints, cycle_ints, block_dims):
    valid = column_valid(block_dims)
    masked = jnp.where(valid[None, :], amplitudes, jnp.zeros((), amplitudes.dtype))
    left_side = masked.astype(jnp.float32)
    block_width = BS * BS

    def column_block(block_index):
        piece_ints = lax.dynamic_slice_in_dim(ladder_ints, (block_index * block_width).astype(jnp.int32), block_width, 1).astype(jnp.float32)
        return jnp.dot(left_side, piece_ints, precision=lax.Precision.HIGHEST)

    blocks_out = lax.map(column_block, jnp.arange(NSB, dtype=jnp.int32))
    ladder = jnp.transpose(blocks_out, (1, 0, 2)).reshape(IJ, NSB * block_width)
    ladder_res = jnp.where(valid[None, :], ladder, jnp.zeros((), ladder.dtype)).astype(jnp.bfloat16)
    row_virtual = jnp.arange(IW * BS, dtype=jnp.int32) % BS
    column_virtual = jnp.arange(JW * BS, dtype=jnp.int32) % BS
    results = []
    for sector_block in range(NSB):
        amp_block = masked[:, sector_block * block_width:(sector_block + 1) * block_width]
        amp_block = amp_block.reshape(NO, JW, BS, BS).astype(jnp.float32)
        cycle_term = jnp.einsum("cke,kjcd->ejd", cycle_ints[sector_block].astype(jnp.float32), amp_block, precision=lax.Precision.HIGHEST)
        cycle_term = cycle_term.reshape(IW * BS, JW * BS)
        allowed = (row_virtual[:, None] < block_dims[sector_block, 0]) & (column_virtual[None, :] < block_dims[sector_block, 1])
        results.append(jnp.where(allowed, cycle_term, jnp.zeros((), cycle_term.dtype)).astype(jnp.bfloat16))
    cycle_res = jnp.stack(results, 0)
    return (ladder_res, cycle_res)
```

```python
import jax
import jax.numpy as jnp
from jax import lax
from jax.sharding import PartitionSpec as P

BS = 64


def block_sizes(block_dims, owner):
    blocks_count = block_dims.shape[0]
    select = owner[:, None] == lax.iota(jnp.int32, blocks_count)[None, :]
    size_first = jnp.sum(jnp.where(select, block_dims[None, :, 0], 0), 1)
    size_second = jnp.sum(jnp.where(select, block_dims[None, :, 1], 0), 1)
    return (size_first, size_second)


def column_valid(block_dims, first_column, column_count):
    column = first_column + lax.iota(jnp.int32, column_count)
    owner = column // (BS * BS)
    size_first, size_second = block_sizes(block_dims, owner)
    return (column // BS % BS < size_first) & (column % BS < size_second)


def local(amplitudes, ladder_ints, cycle_ints, block_dims):
    slab_index = lax.axis_index("slab")
    blk_index = lax.axis_index("blk")
    block_width = amplitudes.shape[1]
    valid = column_valid(block_dims, slab_index * block_width, block_width)
    masked = jnp.where(valid[None, :], amplitudes, jnp.zeros((), amplitudes.dtype))
    gathered = lax.all_gather(masked, "blk", axis=0, tiled=True)
    pair_rows = gathered.shape[0]
    ladder_sum = lax.psum_scatter(
        jnp.dot(gathered, ladder_ints, preferred_element_type=jnp.float32),
        "slab",
        scatter_dimension=0,
        tiled=True,
    )
    out_columns = ladder_ints.shape[1]
    out_valid = column_valid(block_dims, blk_index * out_columns, out_columns)
    ladder_res = jnp.where(out_valid[None, :], ladder_sum, 0.0).astype(jnp.bfloat16)
    occupied = cycle_ints.shape[2]
    j_window = pair_rows // occupied
    c_part = cycle_ints.shape[1]
    columns = lax.dynamic_slice_in_dim(gathered, blk_index * (c_part * BS), c_part * BS, 1)
    amp_part = columns.reshape(occupied, j_window, c_part, BS)
    cycle_term = jnp.einsum(
        "cke,kjcd->ejd", cycle_ints[0], amp_part, preferred_element_type=jnp.float32
    )
    cycle_term = cycle_term.reshape(cycle_term.shape[0], j_window * BS)
    cycle_sum = lax.psum_scatter(cycle_term, "blk", scatter_dimension=0, tiled=True)
    local_rows = cycle_sum.shape[0]
    own_block = jnp.full((1,), slab_index, jnp.int32)
    size_first, size_second = block_sizes(block_dims, own_block)
    row_virtual = (blk_index * local_rows + lax.iota(jnp.int32, local_rows)) % BS
    column_virtual = lax.iota(jnp.int32, j_window * BS) % BS
    allowed = (row_virtual[:, None] < size_first[0]) & (column_virtual[None, :] < size_second[0])
    cycle_res = jnp.where(allowed, cycle_sum, 0.0).astype(jnp.bfloat16)[None]
    return (ladder_res, cycle_res)


def solution(mesh):
    in_specs = (P("blk", "slab"), P("slab", "blk"), P("slab", "blk", None, None), P())
    out_specs = (P("slab", "blk"), P("slab", "blk", None))
    return jax.shard_map(local, mesh=mesh, in_specs=in_specs, out_specs=out_specs, check_vma=False)
```

```python
import functools

import jax
import jax.numpy as jnp
from jax import lax
from jax.experimental import pallas as pl
from jax.experimental.pallas import tpu as pltpu
from jax.sharding import PartitionSpec as P

BS = 64
NX = 4
NY = 4
NZ = 8
MESH = pl.DeviceIdType.MESH
ROWS = 30
STAGE = 16
HALF = 2048
QUART = 1024
WIDE = 512
ORIGINS = (0, -1, 1, 2)
CODE = 64.0
TOP = 32766.0
REACH = ((4, 3), (3, 4))


def merge(first, second):
    out = []
    for index in range(max(len(first), len(second))):
        if index < len(first):
            out.append(first[index])
        if index < len(second):
            out.append(second[index])
    return out


def kernel(
    amp_hbm, ints_hbm, cyc_hbm, dims_ref, ladder_ref, cycle_ref,
    amp_v, gat, wts, cyc_v, part, sbuf, rbuf, outf, tbl, rhs, lhs, lhs_t, cyc_p, cyc_x, cyc_s, cyc_r,
    loc_sem, ag_send, ag_recv, cc_send, cc_recv, rs_send, rs_recv, cy_send, cy_recv,
):
    blk = lax.axis_index("blk")
    z = lax.axis_index("slab")
    core = lax.rem(blk, 2)
    here = blk // 2
    x = here // NY
    y = lax.rem(here, NY)
    other = 1 - core

    amp_copy = pltpu.make_async_copy(amp_hbm, amp_v, loc_sem.at[0])
    amp_copy.start()
    wts_copies = []
    for piece in range(8):
        rows = pl.ds(piece * 512, 512)
        wts_copies.append(pltpu.make_async_copy(ints_hbm.at[rows], wts.at[rows], loc_sem.at[2 + piece]))
    cyc_copy = pltpu.make_async_copy(cyc_hbm, cyc_v, loc_sem.at[1])

    def chip(dx, dy):
        return lax.rem(x + dx + NX, NX) * NY + lax.rem(y + dy + NY, NY)

    def rel(du, dv):
        dx = (1 - core) * du + core * dv
        dy = core * du + (1 - core) * dv
        return lax.rem(x + dx + NX, NX) * NY + lax.rem(y + dy + NY, NY)

    def device(place, which):
        return (place * 2 + which, z)

    def along(step):
        return (blk, lax.rem(z + step + NZ, NZ))

    shifts = [(dx, dy) for dx in range(NX) for dy in range(NY) if (dx, dy) != (0, 0)]

    barrier = pltpu.get_barrier_semaphore()
    pl.semaphore_signal(barrier, inc=1, device_id=device(here, other), device_id_type=MESH)
    for dx, dy in shifts:
        pl.semaphore_signal(barrier, inc=1, device_id=device(chip(dx, dy), core), device_id_type=MESH)
    for step in (1, -1):
        pl.semaphore_signal(barrier, inc=1, device_id=along(step), device_id_type=MESH)

    size_c = dims_ref[z, 0]
    size_d = dims_ref[z, 1]
    amp_copy.wait()
    lane = lax.broadcasted_iota(jnp.int32, (STAGE, 2 * HALF), 1)
    valid = (lane // BS < size_c) & (lax.rem(lane, BS) < size_d)
    zero = jnp.zeros((), jnp.float32)
    for h in range(2):
        count = min(STAGE, ROWS - h * STAGE)
        mine = amp_v[h * STAGE:h * STAGE + count, :].astype(jnp.float32)
        if count < STAGE:
            mine = jnp.concatenate([mine, jnp.zeros((STAGE - count, 2 * HALF), jnp.float32)], 0)
        gat[h, pl.ds(pl.multiple_of(blk * STAGE, STAGE), STAGE), :] = jnp.where(valid, mine, zero).astype(jnp.bfloat16)

    pl.semaphore_wait(barrier, len(shifts) + 3)

    pending = []

    def send(src, dst, send_sem, recv_sem, to):
        copy = pltpu.make_async_remote_copy(
            src_ref=src, dst_ref=dst, send_sem=send_sem, recv_sem=recv_sem, device_id=to, device_id_type=MESH
        )
        copy.start()
        pending.append(copy)

    def arrived(dst, send_sem, recv_sem):
        pltpu.make_async_remote_copy(
            src_ref=dst, dst_ref=dst, send_sem=send_sem, recv_sem=recv_sem,
            device_id=device(here, other), device_id_type=MESH,
        ).wait_recv()

    def block(h, place, piece):
        rows = pl.ds(pl.multiple_of(place * 32, 32), 32)
        if piece is None:
            cols = pl.ds(pl.multiple_of(core * HALF, HALF), HALF)
        else:
            cols = pl.ds(pl.multiple_of(core * HALF + piece * QUART, QUART), QUART)
        return gat.at[h, rows, cols]

    counters = {}

    def next_of(key):
        counters[key] = counters.get(key, -1) + 1
        return counters[key]

    U_M, U_P, U2_0, U2_1 = 0, 1, 2, 3

    def slot_v(kind, origin):
        return 4 + kind * 4 + ORIGINS.index(origin)

    def push(h, place, piece, slot, to):
        ref = block(h, place, piece)
        send(ref, ref, ag_send.at[h, next_of(("ag", h))], ag_recv.at[h, slot], device(to, core))

    def got(h, place, piece, slot):
        arrived(block(h, place, piece), ag_send.at[h, 0], ag_recv.at[h, slot])

    def share(h, place):
        index = next_of(("cc", h))
        ref = block(h, place, None)
        send(ref, ref, cc_send.at[h, index], cc_recv.at[h, index], device(here, other))

    def up(h, origin, piece_place):
        push(h, piece_place, None, slot_v(0, origin), rel(0, 1))
        push(h, piece_place, None, slot_v(1, origin), rel(0, -1))

    def swap(h):
        index = next_of(("cc", h))
        ref = gat.at[h, pl.ds(pl.multiple_of(blk * STAGE, STAGE), STAGE)]
        send(ref, ref, cc_send.at[h, index], cc_recv.at[h, index], device(here, other))

    def swapped(h):
        ref = gat.at[h, pl.ds(pl.multiple_of((here * 2 + other) * STAGE, STAGE), STAGE)]
        arrived(ref, cc_send.at[h, 0], cc_recv.at[h, 0])

    def own(h):
        push(h, here, None, U_M, rel(1, 0))
        push(h, here, None, U_P, rel(-1, 0))
        up(h, 0, here)

    def first_hop(h, sign):
        place = rel(-sign, 0)
        got(h, place, None, U_M if sign > 0 else U_P)
        if sign > 0:
            push(h, place, 0, U2_0, rel(1, 0))
        else:
            push(h, place, 1, U2_1, rel(-1, 0))
        up(h, -sign, place)
        share(h, place)

    def second_hop(h):
        place = rel(2, 0)
        got(h, place, 0, U2_0)
        got(h, place, 1, U2_1)
        up(h, 2, place)
        share(h, place)

    def column_hop(h, origin):
        low = rel(origin, -1)
        got(h, low, None, slot_v(0, origin))
        push(h, low, 0, slot_v(2, origin), rel(0, 1))
        share(h, low)
        high = rel(origin, 1)
        got(h, high, None, slot_v(1, origin))
        push(h, high, 1, slot_v(3, origin), rel(0, -1))
        share(h, high)

    def column_end(h, origin):
        far = rel(origin, 2)
        got(h, far, 0, slot_v(2, origin))
        got(h, far, 1, slot_v(3, origin))
        share(h, far)

    def shared(h):
        for index in range(1, 16):
            arrived(block(h, here, None), cc_send.at[h, 0], cc_recv.at[h, index])

    def gather_steps(h):
        steps = [
            functools.partial(first_hop, h, 1),
            functools.partial(first_hop, h, -1),
            functools.partial(column_hop, h, 0),
            functools.partial(second_hop, h),
            functools.partial(column_hop, h, -1),
            functools.partial(column_hop, h, 1),
            functools.partial(column_end, h, 0),
            functools.partial(column_hop, h, 2),
        ]
        return steps

    def gather_ends(h):
        for origin in (-1, 1, 2):
            column_end(h, origin)
        shared(h)

    def product(h, half):
        def tile(n, carry):
            cols = pl.ds(pl.multiple_of(half * WIDE + n * 256, 256), 256)
            part[h, :, cols] = jnp.dot(gat[h], wts[:, cols], preferred_element_type=jnp.float32)
            return carry

        lax.fori_loop(0, 2, tile, 0)

    def chunk(h, half, dest, lb):
        rows = pl.ds(pl.multiple_of(dest * 64, 64), 64)
        return part[h, rows, half * WIDE + lb * 128:half * WIDE + (lb + 1) * 128]

    def decode(h, way, half, t):
        codes = rbuf[h, way, half, t, 256:272, :].astype(jnp.int32).astype(jnp.float32)
        scales = jnp.exp2(codes * (1.0 / CODE)) * (1.0 / TOP)
        pieces = []
        for lb in range(4):
            q = rbuf[h, way, half, t, lb * 64:(lb + 1) * 64, :].astype(jnp.int32).astype(jnp.float32)
            pieces.append(q * scales[lb:lb + 1, :])
        return pieces

    def landed(h, way, half, t):
        arrived(rbuf.at[h, way, half, t], rs_send.at[h, way, half, 0], rs_recv.at[h, way, half, t])

    def hop(h, way, half, t):
        sign = 1 if way == 0 else -1
        reach = REACH[half][way]
        if t >= reach:
            return
        dest = lax.rem(z + sign * (reach - t) + NZ, NZ)
        if t > 0:
            landed(h, way, half, t - 1)
            before = decode(h, way, half, t - 1)
        row = lax.broadcasted_iota(jnp.int32, (16, 128), 0)
        codes = jnp.zeros((16, 128), jnp.float32)
        for lb in range(4):
            v = chunk(h, half, dest, lb)
            if t > 0:
                v = v + before[lb]
            top = jnp.maximum(jnp.max(jnp.abs(v), axis=0, keepdims=True), 1e-36)
            code = jnp.ceil(jnp.log2(top) * CODE)
            q = jnp.round(v * (jnp.exp2(code * (-1.0 / CODE)) * TOP))
            sbuf[h, way, half, t, lb * 64:(lb + 1) * 64, :] = q.astype(jnp.int32).astype(jnp.int16)
            codes = jnp.where(row == lb, code, codes)
        sbuf[h, way, half, t, 256:272, :] = codes.astype(jnp.int32).astype(jnp.int16)
        send(sbuf.at[h, way, half, t], rbuf.at[h, way, half, t], rs_send.at[h, way, half, t],
             rs_recv.at[h, way, half, t], along(sign))

    def hops(h, half, t):
        hop(h, 0, half, t)
        hop(h, 1, half, t)

    q_out = blk // 4
    out_a = dims_ref[q_out, 0]
    out_b = dims_ref[q_out, 1]

    def settle(h, half):
        landed(h, 0, half, REACH[half][0] - 1)
        landed(h, 1, half, REACH[half][1] - 1)
        plus = decode(h, 0, half, REACH[half][0] - 1)
        minus = decode(h, 1, half, REACH[half][1] - 1)
        for lb in range(4):
            start = half * WIDE + lb * 128
            column = lax.broadcasted_iota(jnp.int32, (64, 128), 1) + start
            a = lax.rem(blk, 4) * 16 + column // BS
            keep = (a < out_a) & (lax.rem(column, BS) < out_b)
            total = chunk(h, half, z, lb) + plus[lb] + minus[lb]
            total = jnp.where(keep, total, 0.0)
            for g in range(4):
                count = min(STAGE, ROWS - h * STAGE)
                row0 = g * ROWS + h * STAGE
                outf[row0:row0 + count, start:start + 128] = total[g * STAGE:g * STAGE + count, :]

    def cycle_left():
        cyc_copy.wait()
        lhs[...] = jnp.zeros_like(lhs)
        for cc in range(2):
            lhs[cc * 128:cc * 128 + 120, :] = cyc_v[cc]
        lhs_t[...] = lhs[...].T

    def cycle_rows(h):
        cols = pl.ds(pl.multiple_of(blk * 128, 128), 128)
        count = min(STAGE, ROWS - h * STAGE)
        for src in range(32):
            rows = gat[h, src * STAGE:(src + 1) * STAGE, cols].astype(jnp.float32)
            tbl[src * ROWS + h * STAGE:src * ROWS + h * STAGE + count, :] = rows[:count]

    def cycle_product():
        first = lax.broadcasted_iota(jnp.int32, (120, 128), 1) < 64
        rhs[...] = jnp.zeros_like(rhs)
        for pair in range(4):
            even = tbl[pl.ds(2 * pair, 120, stride=8), :]
            odd = tbl[pl.ds(2 * pair + 1, 120, stride=8), :]
            cols = slice(pair * 128, (pair + 1) * 128)
            rhs[0:120, cols] = jnp.where(first, even, pltpu.roll(odd, 64, 1)).astype(jnp.bfloat16)
            rhs[128:248, cols] = jnp.where(first, pltpu.roll(even, 64, 1), odd).astype(jnp.bfloat16)
        for n in range(2):
            cols = slice(n * 256, (n + 1) * 256)
            term = jnp.dot(lhs_t[...], rhs[:, cols], preferred_element_type=jnp.float32)
            cyc_p[:, :, :, cols] = term.reshape(16, 2, 16, 256)
        send(cyc_p.at[:, other], cyc_x, cy_send.at[0], cy_recv.at[0], device(here, other))

    def cycle_spread():
        arrived(cyc_x, cy_send.at[0], cy_recv.at[0])
        cyc_s[...] = cyc_p[:, core] + cyc_x[...]
        for index, (dx, dy) in enumerate(shifts):
            to = chip(dx, dy)
            send(cyc_s.at[to], cyc_r.at[index], cy_send.at[1 + index], cy_recv.at[1 + index], device(to, core))

    def cycle_settle():
        total = cyc_s[here]
        for index in range(len(shifts)):
            arrived(cyc_r.at[index], cy_send.at[0], cy_recv.at[1 + index])
            total = total + cyc_r[index]
        size_a = dims_ref[z, 0]
        size_b = dims_ref[z, 1]
        a = lax.rem(blk, 4) * 16 + lax.broadcasted_iota(jnp.int32, (16, 512), 0)
        b = lax.rem(lax.broadcasted_iota(jnp.int32, (16, 512), 1), BS)
        cycle_ref[...] = jnp.where((a < size_a) & (b < size_b), total, 0.0).astype(jnp.bfloat16)

    swap(0)
    swap(1)
    swapped(0)
    own(0)
    for copy in wts_copies:
        copy.start()
    cyc_copy.start()
    for step in gather_steps(0):
        step()
    cycle_left()
    swapped(1)
    own(1)
    gather_ends(0)
    for copy in wts_copies:
        copy.wait()

    def ladder_steps(h):
        return [
            functools.partial(product, h, 0),
            functools.partial(hops, h, 0, 0),
            functools.partial(product, h, 1),
            functools.partial(hops, h, 1, 0),
            functools.partial(hops, h, 0, 1),
            functools.partial(hops, h, 1, 1),
            functools.partial(hops, h, 0, 2),
            functools.partial(hops, h, 1, 2),
            functools.partial(hops, h, 0, 3),
            functools.partial(hops, h, 1, 3),
        ]

    for step in merge(ladder_steps(0), gather_steps(1)):
        step()
    cycle_rows(0)
    gather_ends(1)
    product(1, 0)
    hops(1, 0, 0)
    product(1, 1)
    hops(1, 1, 0)
    cycle_rows(1)
    cycle_product()
    hops(1, 0, 1)
    hops(1, 1, 1)
    cycle_spread()
    settle(0, 0)
    settle(0, 1)
    hops(1, 0, 2)
    hops(1, 1, 2)
    hops(1, 0, 3)
    hops(1, 1, 3)
    cycle_settle()
    settle(1, 0)
    settle(1, 1)
    ladder_ref[...] = outf[...].astype(jnp.bfloat16)
    for copy in pending:
        copy.wait_send()


def local(amplitudes, ladder_ints, cycle_ints, block_dims):
    any_space = pl.BlockSpec(memory_space=pl.ANY)
    vmem = pl.BlockSpec(memory_space=pltpu.VMEM)
    dma = pltpu.SemaphoreType.DMA
    ladder, cycle = pl.pallas_call(
        kernel,
        out_shape=(
            jax.ShapeDtypeStruct((120, 1024), jnp.bfloat16),
            jax.ShapeDtypeStruct((16, 512), jnp.bfloat16),
        ),
        in_specs=[any_space, any_space, any_space, pl.BlockSpec(memory_space=pltpu.SMEM)],
        out_specs=(vmem, vmem),
        scratch_shapes=[
            pltpu.VMEM((ROWS, 2 * HALF), jnp.bfloat16),
            pltpu.VMEM((2, 512, 4096), jnp.bfloat16),
            pltpu.VMEM((4096, 1024), jnp.bfloat16),
            pltpu.VMEM((2, 120, 512), jnp.bfloat16),
            pltpu.VMEM((2, 512, 1024), jnp.float32),
            pltpu.VMEM((2, 2, 2, 4, 272, 128), jnp.int16),
            pltpu.VMEM((2, 2, 2, 4, 272, 128), jnp.int16),
            pltpu.VMEM((120, 1024), jnp.float32),
            pltpu.VMEM((960, 128), jnp.float32),
            pltpu.VMEM((256, 512), jnp.bfloat16),
            pltpu.VMEM((256, 512), jnp.bfloat16),
            pltpu.VMEM((512, 256), jnp.bfloat16),
            pltpu.VMEM((16, 2, 16, 512), jnp.float32),
            pltpu.VMEM((16, 16, 512), jnp.float32),
            pltpu.VMEM((16, 16, 512), jnp.float32),
            pltpu.VMEM((15, 16, 512), jnp.float32),
            dma((10,)),
            dma((2, 20)),
            dma((2, 20)),
            dma((2, 16)),
            dma((2, 16)),
            dma((2, 2, 2, 4)),
            dma((2, 2, 2, 4)),
            dma((16,)),
            dma((16,)),
        ],
        compiler_params=pltpu.CompilerParams(
            collective_id=0, has_side_effects=True, vmem_limit_bytes=56 << 20
        ),
    )(amplitudes, ladder_ints, cycle_ints[0], block_dims)
    return ladder, cycle[None]


def solution(mesh):
    in_specs = (P("blk", "slab"), P("slab", "blk"), P("slab", "blk", None, None), P())
    out_specs = (P("slab", "blk"), P("slab", "blk", None))
    return jax.shard_map(local, mesh=mesh, in_specs=in_specs, out_specs=out_specs, check_vma=False)
```

```python
import jax
import jax.numpy as jnp
from jax import lax
from jax.experimental import pallas as pl
from jax.experimental.pallas import tpu as pltpu
from jax.sharding import PartitionSpec as P

BS = 64
NX = 4
NY = 4
NZ = 8
MESH = pl.DeviceIdType.MESH
ROWS = 30
STAGE = 8
STAGES = 4
BLOCK = 16
CHUNK = 32
HALF = 2048
QUART = 1024
WIDE = 512
STRAIGHT = (0, 3)
ORIGINS = (0, -1, 1, 2)
CODE = 64.0
TOP = 32766.0
REACH = ((4, 3), (3, 4))


def kernel(
    amp_hbm, ints_hbm, cyc_hbm, dims_ref, ladder_ref, cycle_ref,
    amp_v, mine_v, their_v, gat, wts, cyc_v, part, sbuf, rbuf, outf, tbl, rhs, lhs, lhs_t, cyc_p, cyc_x, cyc_s, cyc_r,
    loc_sem, sw_send, sw_recv, ag_send, ag_recv, cc_send, cc_recv, rs_send, rs_recv, cy_send, cy_recv,
):
    blk = lax.axis_index("blk")
    z = lax.axis_index("slab")
    core = lax.rem(blk, 2)
    here = blk // 2
    x = here // NY
    y = lax.rem(here, NY)
    other = 1 - core

    amp_copy = pltpu.make_async_copy(amp_hbm, amp_v, loc_sem.at[0])
    amp_copy.start()
    wts_copies = []
    for piece in range(8):
        rows = pl.ds(piece * 512, 512)
        wts_copies.append(pltpu.make_async_copy(ints_hbm.at[rows], wts.at[rows], loc_sem.at[2 + piece]))
    cyc_copy = pltpu.make_async_copy(cyc_hbm, cyc_v, loc_sem.at[1])
    for copy in wts_copies:
        copy.start()
    cyc_copy.start()

    def chip(dx, dy):
        return lax.rem(x + dx + NX, NX) * NY + lax.rem(y + dy + NY, NY)

    def rel(du, dv):
        dx = (1 - core) * du + core * dv
        dy = core * du + (1 - core) * dv
        return lax.rem(x + dx + NX, NX) * NY + lax.rem(y + dy + NY, NY)

    def device(place, which):
        return (place * 2 + which, z)

    def along(step):
        return (blk, lax.rem(z + step + NZ, NZ))

    shifts = [(dx, dy) for dx in range(NX) for dy in range(NY) if (dx, dy) != (0, 0)]

    barrier = pltpu.get_barrier_semaphore()
    pl.semaphore_signal(barrier, inc=1, device_id=device(here, other), device_id_type=MESH)
    for dx, dy in shifts:
        pl.semaphore_signal(barrier, inc=1, device_id=device(chip(dx, dy), core), device_id_type=MESH)
    for step in (1, -1):
        pl.semaphore_signal(barrier, inc=1, device_id=along(step), device_id_type=MESH)

    size_c = dims_ref[0, z]
    size_d = dims_ref[1, z]
    amp_copy.wait()
    lane = lax.broadcasted_iota(jnp.int32, (ROWS, 2 * HALF), 1)
    valid = (lane // BS < size_c) & (lax.rem(lane, BS) < size_d)
    masked = jnp.where(valid, amp_v[...].astype(jnp.float32), 0.0).astype(jnp.bfloat16)
    mine_v[STAGE * STAGES - BLOCK:, :] = jnp.zeros((BLOCK, 2 * HALF), jnp.bfloat16)
    mine_v[0:ROWS, :] = masked

    pl.semaphore_wait(barrier, len(shifts) + 3)

    pending = []

    def send(src, dst, send_sem, recv_sem, to):
        copy = pltpu.make_async_remote_copy(
            src_ref=src, dst_ref=dst, send_sem=send_sem, recv_sem=recv_sem, device_id=to, device_id_type=MESH
        )
        copy.start()
        pending.append(copy)

    def arrived(dst, send_sem, recv_sem):
        pltpu.make_async_remote_copy(
            src_ref=dst, dst_ref=dst, send_sem=send_sem, recv_sem=recv_sem,
            device_id=device(here, other), device_id_type=MESH,
        ).wait_recv()

    def block(h, place, piece):
        rows = pl.ds(pl.multiple_of(place * BLOCK, BLOCK), BLOCK)
        if piece is None:
            cols = pl.ds(pl.multiple_of(core * HALF, HALF), HALF)
        else:
            cols = pl.ds(pl.multiple_of(core * HALF + piece * QUART, QUART), QUART)
        return gat.at[h, rows, cols]

    counters = {}

    def next_of(key):
        counters[key] = counters.get(key, -1) + 1
        return counters[key]

    U_M, U_P, U2_0, U2_1 = 0, 1, 2, 3

    def slot_v(kind, origin):
        return 4 + kind * 4 + ORIGINS.index(origin)

    def push(h, place, piece, slot, to):
        ref = block(h, place, piece)
        send(ref, ref, ag_send.at[h, next_of(("ag", h))], ag_recv.at[h, slot], device(to, core))

    def got(h, place, piece, slot):
        arrived(block(h, place, piece), ag_send.at[h, 0], ag_recv.at[h, slot])

    def share(h, place):
        index = next_of(("cc", h))
        ref = block(h, place, None)
        send(ref, ref, cc_send.at[h, index], cc_recv.at[h, index], device(here, other))

    def up(h, origin, piece_place):
        push(h, piece_place, None, slot_v(0, origin), rel(0, 1))
        push(h, piece_place, None, slot_v(1, origin), rel(0, -1))

    def swap(part_of):
        rows = pl.ds(part_of * BLOCK, BLOCK)
        send(mine_v.at[rows], their_v.at[rows], sw_send.at[part_of], sw_recv.at[part_of], device(here, other))

    def swapped(part_of):
        rows = pl.ds(part_of * BLOCK, BLOCK)
        arrived(their_v.at[rows], sw_send.at[part_of], sw_recv.at[part_of])

    def assemble(h):
        pair = slice(h // 2 * BLOCK, h // 2 * BLOCK + BLOCK)
        start = h % 2 * STAGE
        mine = mine_v[pair, :].astype(jnp.float32)[start:start + STAGE]
        theirs = their_v[pair, :].astype(jnp.float32)[start:start + STAGE]
        low = jnp.where(core == 0, mine, theirs)
        high = jnp.where(core == 0, theirs, mine)
        gat[h, pl.ds(pl.multiple_of(here * BLOCK, BLOCK), BLOCK), :] = jnp.concatenate([low, high], 0).astype(jnp.bfloat16)

    def own(h):
        push(h, here, None, U_M, rel(1, 0))
        push(h, here, None, U_P, rel(-1, 0))
        if h in STRAIGHT:
            push(h, here, None, U2_0, rel(2, 0))
        up(h, 0, here)

    def first_hop(h, sign):
        place = rel(-sign, 0)
        got(h, place, None, U_M if sign > 0 else U_P)
        if h in STRAIGHT:
            pass
        elif sign > 0:
            push(h, place, 0, U2_0, rel(1, 0))
        else:
            push(h, place, 1, U2_1, rel(-1, 0))
        up(h, -sign, place)
        share(h, place)

    def second_hop(h):
        place = rel(2, 0)
        if h in STRAIGHT:
            got(h, place, None, U2_0)
        else:
            got(h, place, 0, U2_0)
            got(h, place, 1, U2_1)
        up(h, 2, place)
        share(h, place)

    def column_low(h, origin):
        low = rel(origin, -1)
        got(h, low, None, slot_v(0, origin))
        push(h, low, 0, slot_v(2, origin), rel(0, 1))
        share(h, low)

    def column_high(h, origin):
        high = rel(origin, 1)
        got(h, high, None, slot_v(1, origin))
        push(h, high, 1, slot_v(3, origin), rel(0, -1))
        share(h, high)

    def column_end(h, origin):
        far = rel(origin, 2)
        got(h, far, 0, slot_v(2, origin))
        got(h, far, 1, slot_v(3, origin))
        share(h, far)

    def shared(h):
        for index in range(15):
            arrived(block(h, here, None), cc_send.at[h, 0], cc_recv.at[h, index])

    def product(h, half):
        cols = slice(half * WIDE, (half + 1) * WIDE)
        part[h, :, cols] = jnp.dot(gat[h], wts[:, cols], preferred_element_type=jnp.float32)

    def chunk(h, half, dest, lb):
        rows = pl.ds(pl.multiple_of(dest * CHUNK, CHUNK), CHUNK)
        return part[h, rows, half * WIDE + lb * 128:half * WIDE + (lb + 1) * 128]

    def decode(h, way, half, t):
        codes = rbuf[h, way, half, t, 4 * CHUNK:, :].astype(jnp.int32).astype(jnp.float32)
        scales = jnp.exp2(codes * (1.0 / CODE)) * (1.0 / TOP)
        pieces = []
        for lb in range(4):
            q = rbuf[h, way, half, t, lb * CHUNK:(lb + 1) * CHUNK, :].astype(jnp.int32).astype(jnp.float32)
            pieces.append(q * scales[lb:lb + 1, :])
        return pieces

    def landed(h, way, half, t):
        arrived(rbuf.at[h, way, half, t], rs_send.at[h, way, half, 0], rs_recv.at[h, way, half, t])

    def hop(h, way, half, t):
        sign = 1 if way == 0 else -1
        reach = REACH[half][way]
        if t >= reach:
            return
        dest = lax.rem(z + sign * (reach - t) + NZ, NZ)
        if t > 0:
            landed(h, way, half, t - 1)
            before = decode(h, way, half, t - 1)
        row = lax.broadcasted_iota(jnp.int32, (8, 128), 0)
        codes = jnp.zeros((8, 128), jnp.float32)
        for lb in range(4):
            v = chunk(h, half, dest, lb)
            if t > 0:
                v = v + before[lb]
            top = jnp.maximum(jnp.max(jnp.abs(v), axis=0, keepdims=True), 1e-36)
            code = jnp.ceil(jnp.log2(top) * CODE)
            q = jnp.round(v * (jnp.exp2(code * (-1.0 / CODE)) * TOP))
            sbuf[h, way, half, t, lb * CHUNK:(lb + 1) * CHUNK, :] = q.astype(jnp.int32).astype(jnp.int16)
            codes = jnp.where(row == lb, code, codes)
        sbuf[h, way, half, t, 4 * CHUNK:, :] = codes.astype(jnp.int32).astype(jnp.int16)
        send(sbuf.at[h, way, half, t], rbuf.at[h, way, half, t], rs_send.at[h, way, half, t],
             rs_recv.at[h, way, half, t], along(sign))

    def hops(h, half, t):
        hop(h, 0, half, t)
        hop(h, 1, half, t)

    q_out = blk // 4
    out_a = dims_ref[0, q_out]
    out_b = dims_ref[1, q_out]

    def settle(h, half):
        landed(h, 0, half, REACH[half][0] - 1)
        landed(h, 1, half, REACH[half][1] - 1)
        plus = decode(h, 0, half, REACH[half][0] - 1)
        minus = decode(h, 1, half, REACH[half][1] - 1)
        for lb in range(4):
            start = half * WIDE + lb * 128
            column = lax.broadcasted_iota(jnp.int32, (CHUNK, 128), 1) + start
            a = lax.rem(blk, 4) * 16 + column // BS
            keep = (a < out_a) & (lax.rem(column, BS) < out_b)
            total = chunk(h, half, z, lb) + plus[lb] + minus[lb]
            total = jnp.where(keep, total, 0.0)
            count = min(STAGE, ROWS - h * STAGE)
            for g in range(4):
                row0 = g * ROWS + h * STAGE
                outf[row0:row0 + count, start:start + 128] = total[g * STAGE:g * STAGE + count, :]

    def cycle_left():
        cyc_copy.wait()
        lhs[...] = jnp.zeros_like(lhs)
        for cc in range(2):
            lhs[cc * 128:cc * 128 + 120, :] = cyc_v[cc]
        lhs_t[...] = lhs[...].T

    def cycle_rows(h):
        cols = pl.ds(pl.multiple_of(blk * 128, 128), 128)
        count = min(STAGE, ROWS - h * STAGE)
        rows = gat[h, :, cols].astype(jnp.float32)
        for src in range(32):
            tbl[src * ROWS + h * STAGE:src * ROWS + h * STAGE + count, :] = rows[src * STAGE:src * STAGE + count]

    def cycle_product():
        first = lax.broadcasted_iota(jnp.int32, (120, 128), 1) < 64
        rhs[...] = jnp.zeros_like(rhs)
        for pair in range(4):
            even = tbl[pl.ds(2 * pair, 120, stride=8), :]
            odd = tbl[pl.ds(2 * pair + 1, 120, stride=8), :]
            cols = slice(pair * 128, (pair + 1) * 128)
            rhs[0:120, cols] = jnp.where(first, even, pltpu.roll(odd, 64, 1)).astype(jnp.bfloat16)
            rhs[128:248, cols] = jnp.where(first, pltpu.roll(even, 64, 1), odd).astype(jnp.bfloat16)
        for n in range(2):
            cols = slice(n * 256, (n + 1) * 256)
            term = jnp.dot(lhs_t[...], rhs[:, cols], preferred_element_type=jnp.float32)
            cyc_p[:, :, :, cols] = term.reshape(16, 2, 16, 256)
        send(cyc_p.at[:, other], cyc_x, cy_send.at[0], cy_recv.at[0], device(here, other))

    def cycle_spread():
        arrived(cyc_x, cy_send.at[0], cy_recv.at[0])
        cyc_s[...] = cyc_p[:, core] + cyc_x[...]
        for index, (dx, dy) in enumerate(shifts):
            to = chip(dx, dy)
            send(cyc_s.at[to], cyc_r.at[index], cy_send.at[1 + index], cy_recv.at[1 + index], device(to, core))

    def cycle_settle():
        total = cyc_s[here]
        for index in range(len(shifts)):
            arrived(cyc_r.at[index], cy_send.at[0], cy_recv.at[1 + index])
            total = total + cyc_r[index]
        size_a = dims_ref[0, z]
        size_b = dims_ref[1, z]
        a = lax.rem(blk, 4) * 16 + lax.broadcasted_iota(jnp.int32, (16, 512), 0)
        b = lax.rem(lax.broadcasted_iota(jnp.int32, (16, 512), 1), BS)
        cycle_ref[...] = jnp.where((a < size_a) & (b < size_b), total, 0.0).astype(jnp.bfloat16)

    swap(0)
    swap(1)
    swapped(0)
    assemble(0)
    own(0)
    assemble(1)
    swapped(1)
    for h in range(2, STAGES):
        assemble(h)
    own(1)
    first_hop(0, 1)
    first_hop(0, -1)
    column_low(0, 0)
    column_high(0, 0)
    second_hop(0)
    first_hop(1, 1)
    column_low(1, 0)
    first_hop(1, -1)
    column_high(1, 0)
    column_low(0, -1)
    column_high(0, -1)
    column_low(0, 1)
    column_high(0, 1)
    column_end(0, 0)
    column_high(0, 2)
    column_low(0, 2)
    second_hop(1)
    column_low(1, -1)
    column_high(1, -1)
    own(2)
    column_high(1, 1)
    column_low(1, 1)
    column_end(1, 0)
    column_end(0, -1)
    column_end(0, 1)
    column_end(0, 2)
    own(3)
    column_low(1, 2)
    column_high(1, 2)
    shared(0)
    for copy in wts_copies:
        copy.wait()
    cycle_left()
    product(0, 0)
    hops(0, 0, 0)
    column_end(1, -1)
    first_hop(2, 1)
    column_end(1, 1)
    first_hop(2, -1)
    column_low(2, 0)
    column_high(2, 0)
    first_hop(3, 1)
    first_hop(3, -1)
    product(0, 1)
    hops(0, 1, 0)
    column_end(1, 2)
    column_low(3, 0)
    column_high(3, 0)
    second_hop(3)
    cycle_rows(0)
    hops(0, 0, 1)
    second_hop(2)
    column_low(2, -1)
    column_high(2, -1)
    shared(1)
    column_low(2, 1)
    column_high(2, 1)
    product(1, 0)
    hops(0, 1, 1)
    hops(1, 0, 0)
    column_end(2, 0)
    column_low(3, -1)
    column_high(3, -1)
    column_low(3, 1)
    column_high(3, 1)
    hops(0, 0, 2)
    column_end(3, 0)
    column_low(3, 2)
    column_high(3, 2)
    product(1, 1)
    hops(1, 1, 0)
    column_low(2, 2)
    column_high(2, 2)
    column_end(2, -1)
    column_end(2, 1)
    hops(0, 1, 2)
    column_end(3, -1)
    cycle_rows(1)
    column_end(3, 1)
    hops(1, 0, 1)
    column_end(3, 2)
    hops(0, 0, 3)
    shared(3)
    column_end(2, 2)
    hops(1, 1, 1)
    product(3, 0)
    hops(0, 1, 3)
    hops(1, 0, 2)
    hops(3, 0, 0)
    product(3, 1)
    hops(3, 1, 0)
    shared(2)
    hops(1, 1, 2)
    product(2, 0)
    hops(1, 0, 3)
    hops(2, 0, 0)
    product(2, 1)
    hops(2, 1, 0)
    hops(3, 0, 1)
    hops(3, 1, 1)
    settle(0, 0)
    settle(0, 1)
    cycle_rows(2)
    hops(1, 1, 3)
    cycle_rows(3)
    cycle_product()
    hops(2, 0, 1)
    settle(1, 0)
    hops(2, 1, 1)
    hops(3, 0, 2)
    hops(3, 1, 2)
    cycle_spread()
    settle(1, 1)
    hops(2, 0, 2)
    hops(2, 1, 2)
    hops(3, 0, 3)
    hops(3, 1, 3)
    hops(2, 0, 3)
    hops(2, 1, 3)
    cycle_settle()
    settle(3, 0)
    settle(3, 1)
    settle(2, 0)
    settle(2, 1)
    ladder_ref[...] = outf[...].astype(jnp.bfloat16)
    for copy in pending:
        copy.wait_send()


def local(amplitudes, ladder_ints, cycle_ints, block_dims):
    any_space = pl.BlockSpec(memory_space=pl.ANY)
    vmem = pl.BlockSpec(memory_space=pltpu.VMEM)
    dma = pltpu.SemaphoreType.DMA
    ladder, cycle = pl.pallas_call(
        kernel,
        out_shape=(
            jax.ShapeDtypeStruct((120, 1024), jnp.bfloat16),
            jax.ShapeDtypeStruct((16, 512), jnp.bfloat16),
        ),
        in_specs=[any_space, any_space, any_space, pl.BlockSpec(memory_space=pltpu.SMEM)],
        out_specs=(vmem, vmem),
        scratch_shapes=[
            pltpu.VMEM((ROWS, 2 * HALF), jnp.bfloat16),
            pltpu.VMEM((STAGE * STAGES, 2 * HALF), jnp.bfloat16),
            pltpu.VMEM((STAGE * STAGES, 2 * HALF), jnp.bfloat16),
            pltpu.VMEM((STAGES, 256, 4096), jnp.bfloat16),
            pltpu.VMEM((4096, 1024), jnp.bfloat16),
            pltpu.VMEM((2, 120, 512), jnp.bfloat16),
            pltpu.VMEM((STAGES, 256, 1024), jnp.float32),
            pltpu.VMEM((STAGES, 2, 2, 4, 4 * CHUNK + 8, 128), jnp.int16),
            pltpu.VMEM((STAGES, 2, 2, 4, 4 * CHUNK + 8, 128), jnp.int16),
            pltpu.VMEM((120, 1024), jnp.float32),
            pltpu.VMEM((960, 128), jnp.float32),
            pltpu.VMEM((256, 512), jnp.bfloat16),
            pltpu.VMEM((256, 512), jnp.bfloat16),
            pltpu.VMEM((512, 256), jnp.bfloat16),
            pltpu.VMEM((16, 2, 16, 512), jnp.float32),
            pltpu.VMEM((16, 16, 512), jnp.float32),
            pltpu.VMEM((16, 16, 512), jnp.float32),
            pltpu.VMEM((15, 16, 512), jnp.float32),
            dma((10,)),
            dma((2,)),
            dma((2,)),
            dma((STAGES, 20)),
            dma((STAGES, 20)),
            dma((STAGES, 15)),
            dma((STAGES, 15)),
            dma((STAGES, 2, 2, 4)),
            dma((STAGES, 2, 2, 4)),
            dma((16,)),
            dma((16,)),
        ],
        compiler_params=pltpu.CompilerParams(
            collective_id=0, has_side_effects=True, vmem_limit_bytes=56 << 20
        ),
    )(amplitudes, ladder_ints, cycle_ints[0], block_dims.T)
    def hand_over(ladder_in, cycle_in, ladder_out, cycle_out):
        ladder_out[...] = ladder_in[...]
        cycle_out[...] = cycle_in[...]

    ladder, cycle = pl.pallas_call(
        hand_over,
        out_shape=(
            jax.ShapeDtypeStruct((120, 1024), jnp.bfloat16),
            jax.ShapeDtypeStruct((16, 512), jnp.bfloat16),
        ),
        in_specs=[vmem, vmem],
        out_specs=(vmem, vmem),
    )(ladder, cycle)
    return ladder, cycle[None]


def solution(mesh):
    in_specs = (P("blk", "slab"), P("slab", "blk"), P("slab", "blk", None, None), P())
    out_specs = (P("slab", "blk"), P("slab", "blk", None))
    return jax.shard_map(local, mesh=mesh, in_specs=in_specs, out_specs=out_specs, check_vma=False)
```

```python
import jax
import jax.numpy as jnp
from jax import lax
from jax.experimental import pallas as pl
from jax.experimental.pallas import tpu as pltpu
from jax.sharding import PartitionSpec as P

BS = 64
NX = 4
NY = 4
NZ = 8
MESH = pl.DeviceIdType.MESH
ROWS = 30
STAGE = 8
STAGES = 4
BLOCK = 16
CHUNK = 32
HALF = 2048
QUART = 1024
WIDE = 512
STRAIGHT = (0, 2)
FAST = (0, 1, 3)
ORIGINS = (0, -1, 1, 2)
CODE = 64.0
TOP = 32766.0
REACH = ((4, 3), (3, 4))


def kernel(
    amp_hbm, ints_hbm, cyc_hbm, dims_hbm, ladder_ref, cycle_ref,
    dims_ref, amp_v, mine_v, their_v, gat, wts, cyc_v, part, sbuf, rbuf, outf, tbl, rhs, lhs, lhs_t, cyc_p, cyc_x, cyc_s, cyc_r,
    loc_sem, sw_send, sw_recv, ag_send, ag_recv, cc_send, cc_recv, rs_send, rs_recv, cy_send, cy_recv,
):
    blk = lax.axis_index("blk")
    z = lax.axis_index("slab")
    core = lax.rem(blk, 2)
    here = blk // 2
    x = here // NY
    y = lax.rem(here, NY)
    other = 1 - core

    amp_copy = pltpu.make_async_copy(amp_hbm, amp_v, loc_sem.at[0])
    amp_copy.start()
    dims_copy = pltpu.make_async_copy(dims_hbm, dims_ref, loc_sem.at[10])
    dims_copy.start()
    wts_copies = []
    for piece in range(8):
        rows = pl.ds(piece * 512, 512)
        wts_copies.append(pltpu.make_async_copy(ints_hbm.at[rows], wts.at[rows], loc_sem.at[2 + piece]))
    cyc_copy = pltpu.make_async_copy(cyc_hbm, cyc_v, loc_sem.at[1])
    for copy in wts_copies:
        copy.start()
    cyc_copy.start()

    def chip(dx, dy):
        return lax.rem(x + dx + NX, NX) * NY + lax.rem(y + dy + NY, NY)

    def rel(du, dv):
        dx = (1 - core) * du + core * dv
        dy = core * du + (1 - core) * dv
        return lax.rem(x + dx + NX, NX) * NY + lax.rem(y + dy + NY, NY)

    def device(place, which):
        return (place * 2 + which, z)

    def along(step):
        return (blk, lax.rem(z + step + NZ, NZ))

    shifts = [(dx, dy) for dx in range(NX) for dy in range(NY) if (dx, dy) != (0, 0)]

    barrier = pltpu.get_barrier_semaphore()
    pl.semaphore_signal(barrier, inc=1, device_id=device(here, other), device_id_type=MESH)
    for dx, dy in shifts:
        pl.semaphore_signal(barrier, inc=1, device_id=device(chip(dx, dy), core), device_id_type=MESH)
    for step in (1, -1, 2, -2):
        pl.semaphore_signal(barrier, inc=1, device_id=along(step), device_id_type=MESH)

    dims_copy.wait()
    size_c = dims_ref[0, z]
    size_d = dims_ref[1, z]
    amp_copy.wait()
    lane = lax.broadcasted_iota(jnp.int32, (ROWS, 2 * HALF), 1)
    valid = (lane // BS < size_c) & (lax.rem(lane, BS) < size_d)
    masked = jnp.where(valid, amp_v[...].astype(jnp.float32), 0.0).astype(jnp.bfloat16)
    mine_v[STAGE * STAGES - BLOCK:, :] = jnp.zeros((BLOCK, 2 * HALF), jnp.bfloat16)
    mine_v[0:ROWS, :] = masked

    pl.semaphore_wait(barrier, len(shifts) + 5)

    pending = []

    def send(src, dst, send_sem, recv_sem, to):
        copy = pltpu.make_async_remote_copy(
            src_ref=src, dst_ref=dst, send_sem=send_sem, recv_sem=recv_sem, device_id=to, device_id_type=MESH
        )
        copy.start()
        pending.append(copy)

    def arrived(dst, send_sem, recv_sem):
        pltpu.make_async_remote_copy(
            src_ref=dst, dst_ref=dst, send_sem=send_sem, recv_sem=recv_sem,
            device_id=device(here, other), device_id_type=MESH,
        ).wait_recv()

    def block(h, place, piece):
        rows = pl.ds(pl.multiple_of(place * BLOCK, BLOCK), BLOCK)
        if piece is None:
            cols = pl.ds(pl.multiple_of(core * HALF, HALF), HALF)
        else:
            cols = pl.ds(pl.multiple_of(core * HALF + piece * QUART, QUART), QUART)
        return gat.at[h, rows, cols]

    counters = {}

    def next_of(key):
        counters[key] = counters.get(key, -1) + 1
        return counters[key]

    U_M, U_P, U2_0, U2_1 = 0, 1, 2, 3

    def slot_v(kind, origin):
        return 4 + kind * 4 + ORIGINS.index(origin)

    def push(h, place, piece, slot, to):
        ref = block(h, place, piece)
        send(ref, ref, ag_send.at[h, next_of(("ag", h))], ag_recv.at[h, slot], device(to, core))

    def got(h, place, piece, slot):
        arrived(block(h, place, piece), ag_send.at[h, 0], ag_recv.at[h, slot])

    def share(h, place):
        index = next_of(("cc", h))
        ref = block(h, place, None)
        send(ref, ref, cc_send.at[h, index], cc_recv.at[h, index], device(here, other))

    def up(h, origin, piece_place):
        push(h, piece_place, None, slot_v(0, origin), rel(0, 1))
        push(h, piece_place, None, slot_v(1, origin), rel(0, -1))

    def swap(part_of):
        rows = pl.ds(part_of * BLOCK, BLOCK)
        send(mine_v.at[rows], their_v.at[rows], sw_send.at[part_of], sw_recv.at[part_of], device(here, other))

    def swapped(part_of):
        rows = pl.ds(part_of * BLOCK, BLOCK)
        arrived(their_v.at[rows], sw_send.at[part_of], sw_recv.at[part_of])

    def assemble(h):
        pair = slice(h // 2 * BLOCK, h // 2 * BLOCK + BLOCK)
        start = h % 2 * STAGE
        mine = mine_v[pair, :].astype(jnp.float32)[start:start + STAGE]
        theirs = their_v[pair, :].astype(jnp.float32)[start:start + STAGE]
        low = jnp.where(core == 0, mine, theirs)
        high = jnp.where(core == 0, theirs, mine)
        gat[h, pl.ds(pl.multiple_of(here * BLOCK, BLOCK), BLOCK), :] = jnp.concatenate([low, high], 0).astype(jnp.bfloat16)

    def own(h):
        push(h, here, None, U_M, rel(1, 0))
        push(h, here, None, U_P, rel(-1, 0))
        if h in STRAIGHT:
            push(h, here, None, U2_0, rel(2, 0))
        up(h, 0, here)

    def first_hop(h, sign):
        place = rel(-sign, 0)
        got(h, place, None, U_M if sign > 0 else U_P)
        if h in STRAIGHT:
            pass
        elif sign > 0:
            push(h, place, 0, U2_0, rel(1, 0))
        else:
            push(h, place, 1, U2_1, rel(-1, 0))
        up(h, -sign, place)
        share(h, place)

    def second_hop(h):
        place = rel(2, 0)
        if h in STRAIGHT:
            got(h, place, None, U2_0)
        else:
            got(h, place, 0, U2_0)
            got(h, place, 1, U2_1)
        up(h, 2, place)
        share(h, place)

    def column_low(h, origin):
        low = rel(origin, -1)
        got(h, low, None, slot_v(0, origin))
        push(h, low, 0, slot_v(2, origin), rel(0, 1))
        share(h, low)

    def column_high(h, origin):
        high = rel(origin, 1)
        got(h, high, None, slot_v(1, origin))
        push(h, high, 1, slot_v(3, origin), rel(0, -1))
        share(h, high)

    def column_end(h, origin):
        far = rel(origin, 2)
        got(h, far, 0, slot_v(2, origin))
        got(h, far, 1, slot_v(3, origin))
        share(h, far)

    def shared(h):
        for index in range(15):
            arrived(block(h, here, None), cc_send.at[h, 0], cc_recv.at[h, index])

    def product(h, half):
        cols = slice(half * WIDE, (half + 1) * WIDE)
        part[h, :, cols] = jnp.dot(gat[h], wts[:, cols], preferred_element_type=jnp.float32)

    def chunk(h, half, dest, lb):
        rows = pl.ds(pl.multiple_of(dest * CHUNK, CHUNK), CHUNK)
        return part[h, rows, half * WIDE + lb * 128:half * WIDE + (lb + 1) * 128]

    def decode(h, way, half, t):
        codes = rbuf[h, way, half, t, 4 * CHUNK:, :].astype(jnp.int32).astype(jnp.float32)
        scales = jnp.exp2(codes * (1.0 / CODE)) * (1.0 / TOP)
        pieces = []
        for lb in range(4):
            q = rbuf[h, way, half, t, lb * CHUNK:(lb + 1) * CHUNK, :].astype(jnp.int32).astype(jnp.float32)
            pieces.append(q * scales[lb:lb + 1, :])
        return pieces

    def landed(h, way, half, t):
        arrived(rbuf.at[h, way, half, t], rs_send.at[h, way, half, 0], rs_recv.at[h, way, half, t])

    def emit(h, way, half, slot, ahead, earlier, far):
        sign = 1 if way == 0 else -1
        dest = lax.rem(z + sign * ahead + NZ, NZ)
        before = []
        for known in earlier:
            landed(h, way, half, known)
            before.append(decode(h, way, half, known))
        row = lax.broadcasted_iota(jnp.int32, (8, 128), 0)
        codes = jnp.zeros((8, 128), jnp.float32)
        for lb in range(4):
            v = chunk(h, half, dest, lb)
            for pieces in before:
                v = v + pieces[lb]
            top = jnp.maximum(jnp.max(jnp.abs(v), axis=0, keepdims=True), 1e-36)
            code = jnp.ceil(jnp.log2(top) * CODE)
            q = jnp.round(v * (jnp.exp2(code * (-1.0 / CODE)) * TOP))
            sbuf[h, way, half, slot, lb * CHUNK:(lb + 1) * CHUNK, :] = q.astype(jnp.int32).astype(jnp.int16)
            codes = jnp.where(row == lb, code, codes)
        sbuf[h, way, half, slot, 4 * CHUNK:, :] = codes.astype(jnp.int32).astype(jnp.int16)
        send(sbuf.at[h, way, half, slot], rbuf.at[h, way, half, slot], rs_send.at[h, way, half, slot],
             rs_recv.at[h, way, half, slot], along(sign * far))

    def hop(h, way, half, t):
        reach = REACH[half][way]
        if t < reach:
            emit(h, way, half, t, reach - t, [t - 1] if t > 0 else [], 1)

    def hops(h, half, t):
        if h not in FAST:
            hop(h, 0, half, t)
            hop(h, 1, half, t)
            return
        long = 0 if REACH[half][0] == 4 else 1
        if t == 0:
            emit(h, long, half, 0, 4, [], 1)
            hop(h, 1 - long, half, 0)
            emit(h, long, half, 1, 2, [], 1)
        elif t == 1:
            emit(h, long, half, 2, 3, [0], 2)
            hop(h, 1 - long, half, 1)
        elif t == 2:
            emit(h, long, half, 3, 1, [1, 2], 1)
            hop(h, 1 - long, half, 2)

    q_out = blk // 4
    out_a = dims_ref[0, q_out]
    out_b = dims_ref[1, q_out]

    def settle(h, half):
        landed(h, 0, half, REACH[half][0] - 1)
        landed(h, 1, half, REACH[half][1] - 1)
        plus = decode(h, 0, half, REACH[half][0] - 1)
        minus = decode(h, 1, half, REACH[half][1] - 1)
        for lb in range(4):
            start = half * WIDE + lb * 128
            column = lax.broadcasted_iota(jnp.int32, (CHUNK, 128), 1) + start
            a = lax.rem(blk, 4) * 16 + column // BS
            keep = (a < out_a) & (lax.rem(column, BS) < out_b)
            total = chunk(h, half, z, lb) + plus[lb] + minus[lb]
            total = jnp.where(keep, total, 0.0)
            count = min(STAGE, ROWS - h * STAGE)
            for g in range(4):
                row0 = g * ROWS + h * STAGE
                outf[row0:row0 + count, start:start + 128] = total[g * STAGE:g * STAGE + count, :]

    def cycle_left():
        cyc_copy.wait()
        lhs[...] = jnp.zeros_like(lhs)
        for cc in range(2):
            lhs[cc * 128:cc * 128 + 120, :] = cyc_v[cc]
        lhs_t[...] = lhs[...].T

    def cycle_rows(h):
        cols = pl.ds(pl.multiple_of(blk * 128, 128), 128)
        count = min(STAGE, ROWS - h * STAGE)
        rows = gat[h, :, cols].astype(jnp.float32)
        for src in range(32):
            tbl[src * ROWS + h * STAGE:src * ROWS + h * STAGE + count, :] = rows[src * STAGE:src * STAGE + count]

    def cycle_product():
        first = lax.broadcasted_iota(jnp.int32, (120, 128), 1) < 64
        rhs[...] = jnp.zeros_like(rhs)
        for pair in range(4):
            even = tbl[pl.ds(2 * pair, 120, stride=8), :]
            odd = tbl[pl.ds(2 * pair + 1, 120, stride=8), :]
            cols = slice(pair * 128, (pair + 1) * 128)
            rhs[0:120, cols] = jnp.where(first, even, pltpu.roll(odd, 64, 1)).astype(jnp.bfloat16)
            rhs[128:248, cols] = jnp.where(first, pltpu.roll(even, 64, 1), odd).astype(jnp.bfloat16)
        for n in range(2):
            cols = slice(n * 256, (n + 1) * 256)
            term = jnp.dot(lhs_t[...], rhs[:, cols], preferred_element_type=jnp.float32)
            cyc_p[:, :, :, cols] = term.reshape(16, 2, 16, 256)
        send(cyc_p.at[:, other], cyc_x, cy_send.at[0], cy_recv.at[0], device(here, other))

    def cycle_spread():
        arrived(cyc_x, cy_send.at[0], cy_recv.at[0])
        cyc_s[...] = cyc_p[:, core] + cyc_x[...]
        for index, (dx, dy) in enumerate(shifts):
            to = chip(dx, dy)
            send(cyc_s.at[to], cyc_r.at[index], cy_send.at[1 + index], cy_recv.at[1 + index], device(to, core))

    def cycle_settle():
        total = cyc_s[here]
        for index in range(len(shifts)):
            arrived(cyc_r.at[index], cy_send.at[0], cy_recv.at[1 + index])
            total = total + cyc_r[index]
        size_a = dims_ref[0, z]
        size_b = dims_ref[1, z]
        a = lax.rem(blk, 4) * 16 + lax.broadcasted_iota(jnp.int32, (16, 512), 0)
        b = lax.rem(lax.broadcasted_iota(jnp.int32, (16, 512), 1), BS)
        cycle_ref[...] = jnp.where((a < size_a) & (b < size_b), total, 0.0).astype(jnp.bfloat16)

    swap(0)
    swap(1)
    swapped(0)
    assemble(0)
    own(0)
    assemble(1)
    swapped(1)
    for h in range(2, STAGES):
        assemble(h)
    own(1)
    first_hop(0, 1)
    first_hop(0, -1)
    column_low(0, 0)
    column_high(0, 0)
    second_hop(0)
    column_low(1, 0)
    column_high(1, 0)
    first_hop(1, 1)
    first_hop(1, -1)
    column_low(0, -1)
    column_high(0, -1)
    column_low(0, 1)
    column_high(0, 1)
    column_end(0, 0)
    column_high(0, 2)
    column_low(0, 2)
    own(2)
    second_hop(1)
    column_end(1, 0)
    column_low(1, -1)
    column_high(1, -1)
    column_low(1, 1)
    column_high(1, 1)
    own(3)
    column_end(0, -1)
    column_end(0, 1)
    column_end(0, 2)
    first_hop(2, 1)
    first_hop(2, -1)
    shared(0)
    column_low(2, 0)
    column_high(2, 0)
    for copy in wts_copies:
        copy.wait()
    cycle_left()
    product(0, 0)
    hops(0, 0, 0)
    column_low(1, 2)
    column_high(1, 2)
    column_end(1, -1)
    second_hop(2)
    column_end(1, 1)
    first_hop(3, 1)
    first_hop(3, -1)
    product(0, 1)
    hops(0, 1, 0)
    column_low(2, -1)
    column_high(2, -1)
    column_low(2, 1)
    column_high(2, 1)
    column_low(3, 0)
    hops(0, 0, 1)
    column_end(2, 0)
    column_high(3, 0)
    column_end(1, 2)
    cycle_rows(0)
    second_hop(3)
    column_low(2, 2)
    column_high(2, 2)
    shared(1)
    column_low(3, -1)
    column_high(3, -1)
    product(1, 0)
    hops(0, 1, 1)
    hops(1, 0, 0)
    column_end(2, -1)
    hops(0, 0, 2)
    column_end(2, 1)
    column_low(3, 1)
    column_high(3, 1)
    column_end(3, 0)
    column_low(3, 2)
    column_end(2, 2)
    column_high(3, 2)
    product(1, 1)
    hops(1, 1, 0)
    shared(2)
    column_end(3, -1)
    product(2, 0)
    hops(0, 1, 2)
    hops(1, 0, 1)
    hops(2, 0, 0)
    column_end(3, 1)
    column_end(3, 2)
    product(2, 1)
    hops(1, 1, 1)
    hops(2, 1, 0)
    shared(3)
    product(3, 0)
    hops(3, 0, 0)
    product(3, 1)
    hops(1, 0, 2)
    hops(2, 0, 1)
    hops(3, 1, 0)
    settle(0, 0)
    settle(0, 1)
    hops(1, 1, 2)
    cycle_rows(1)
    cycle_rows(2)
    hops(2, 1, 1)
    cycle_rows(3)
    cycle_product()
    hops(3, 0, 1)
    settle(1, 0)
    hops(2, 0, 2)
    hops(3, 1, 1)
    cycle_spread()
    settle(1, 1)
    hops(2, 1, 2)
    hops(3, 0, 2)
    hops(2, 0, 3)
    hops(3, 1, 2)
    hops(2, 1, 3)
    cycle_settle()
    settle(3, 0)
    settle(2, 0)
    settle(3, 1)
    settle(2, 1)
    ladder_ref[...] = outf[...].astype(jnp.bfloat16)
    for copy in pending:
        copy.wait_send()


def local(amplitudes, ladder_ints, cycle_ints, block_dims):
    any_space = pl.BlockSpec(memory_space=pl.ANY)
    vmem = pl.BlockSpec(memory_space=pltpu.VMEM)
    dma = pltpu.SemaphoreType.DMA
    ladder, cycle = pl.pallas_call(
        kernel,
        out_shape=(
            jax.ShapeDtypeStruct((120, 1024), jnp.bfloat16),
            jax.ShapeDtypeStruct((16, 512), jnp.bfloat16),
        ),
        in_specs=[any_space, any_space, any_space, any_space],
        out_specs=(vmem, vmem),
        scratch_shapes=[
            pltpu.SMEM((2, 8), jnp.int32),
            pltpu.VMEM((ROWS, 2 * HALF), jnp.bfloat16),
            pltpu.VMEM((STAGE * STAGES, 2 * HALF), jnp.bfloat16),
            pltpu.VMEM((STAGE * STAGES, 2 * HALF), jnp.bfloat16),
            pltpu.VMEM((STAGES, 256, 4096), jnp.bfloat16),
            pltpu.VMEM((4096, 1024), jnp.bfloat16),
            pltpu.VMEM((2, 120, 512), jnp.bfloat16),
            pltpu.VMEM((STAGES, 256, 1024), jnp.float32),
            pltpu.VMEM((STAGES, 2, 2, 4, 4 * CHUNK + 8, 128), jnp.int16),
            pltpu.VMEM((STAGES, 2, 2, 4, 4 * CHUNK + 8, 128), jnp.int16),
            pltpu.VMEM((120, 1024), jnp.float32),
            pltpu.VMEM((960, 128), jnp.float32),
            pltpu.VMEM((256, 512), jnp.bfloat16),
            pltpu.VMEM((256, 512), jnp.bfloat16),
            pltpu.VMEM((512, 256), jnp.bfloat16),
            pltpu.VMEM((16, 2, 16, 512), jnp.float32),
            pltpu.VMEM((16, 16, 512), jnp.float32),
            pltpu.VMEM((16, 16, 512), jnp.float32),
            pltpu.VMEM((15, 16, 512), jnp.float32),
            dma((11,)),
            dma((2,)),
            dma((2,)),
            dma((STAGES, 20)),
            dma((STAGES, 20)),
            dma((STAGES, 15)),
            dma((STAGES, 15)),
            dma((STAGES, 2, 2, 4)),
            dma((STAGES, 2, 2, 4)),
            dma((16,)),
            dma((16,)),
        ],
        compiler_params=pltpu.CompilerParams(
            collective_id=0, has_side_effects=True, vmem_limit_bytes=56 << 20
        ),
    )(amplitudes, ladder_ints, cycle_ints[0], block_dims.T)
    def hand_over(ladder_in, cycle_in, ladder_out, cycle_out):
        ladder_out[...] = ladder_in[...]
        cycle_out[...] = cycle_in[...]

    ladder, cycle = pl.pallas_call(
        hand_over,
        out_shape=(
            jax.ShapeDtypeStruct((120, 1024), jnp.bfloat16),
            jax.ShapeDtypeStruct((16, 512), jnp.bfloat16),
        ),
        in_specs=[vmem, vmem],
        out_specs=(vmem, vmem),
    )(ladder, cycle)
    return ladder, cycle[None]


def solution(mesh):
    in_specs = (P("blk", "slab"), P("slab", "blk"), P("slab", "blk", None, None), P())
    out_specs = (P("slab", "blk"), P("slab", "blk", None))
    return jax.shard_map(local, mesh=mesh, in_specs=in_specs, out_specs=out_specs, check_vma=False)
```

```python
import jax
import jax.numpy as jnp
from jax import lax
from jax.experimental import pallas as pl
from jax.experimental.pallas import tpu as pltpu
from jax.sharding import PartitionSpec as P

BS = 64
NX = 4
NY = 4
NZ = 8
MESH = pl.DeviceIdType.MESH
ROWS = 30
STAGE = 8
STAGES = 4
BLOCK = 16
CHUNK = 32
HALF = 2048
QUART = 1024
WIDE = 512
STRAIGHT = (0, 2)
FAST = (0, 1, 3)
ORIGINS = (0, -1, 1, 2)
CODE = 64.0
TOP = 32766.0
REACH = ((4, 3), (3, 4))


def kernel(
    amp_hbm, ints_hbm, cyc_hbm, dims_hbm, ladder_ref, cycle_ref,
    dims_ref, amp_v, mine_v, their_v, gat, wts, cyc_v, part, sbuf, rbuf, outf, tbl, rhs, lhs, lhs_t, cyc_p, cyc_x, cyc_s, cyc_r,
    loc_sem, sw_send, sw_recv, ag_send, ag_recv, cc_send, cc_recv, rs_send, rs_recv, cy_send, cy_recv,
):
    blk = lax.axis_index("blk")
    z = lax.axis_index("slab")
    core = lax.rem(blk, 2)
    here = blk // 2
    x = here // NY
    y = lax.rem(here, NY)
    other = 1 - core

    amp_copy = pltpu.make_async_copy(amp_hbm, amp_v, loc_sem.at[0])
    amp_copy.start()
    dims_copy = pltpu.make_async_copy(dims_hbm, dims_ref, loc_sem.at[10])
    dims_copy.start()
    wts_copies = []
    for piece in range(8):
        rows = pl.ds(piece * 512, 512)
        wts_copies.append(pltpu.make_async_copy(ints_hbm.at[rows], wts.at[rows], loc_sem.at[2 + piece]))
    cyc_copy = pltpu.make_async_copy(cyc_hbm, cyc_v, loc_sem.at[1])
    for copy in wts_copies:
        copy.start()
    cyc_copy.start()

    def chip(dx, dy):
        return lax.rem(x + dx + NX, NX) * NY + lax.rem(y + dy + NY, NY)

    def rel(du, dv):
        dx = (1 - core) * du + core * dv
        dy = core * du + (1 - core) * dv
        return lax.rem(x + dx + NX, NX) * NY + lax.rem(y + dy + NY, NY)

    def device(place, which):
        return (place * 2 + which, z)

    def along(step):
        return (blk, lax.rem(z + step + NZ, NZ))

    shifts = [(dx, dy) for dx in range(NX) for dy in range(NY) if (dx, dy) != (0, 0)]

    barrier = pltpu.get_barrier_semaphore()
    pl.semaphore_signal(barrier, inc=1, device_id=device(here, other), device_id_type=MESH)
    for dx, dy in shifts:
        pl.semaphore_signal(barrier, inc=1, device_id=device(chip(dx, dy), core), device_id_type=MESH)
    for step in (1, -1, 2, -2):
        pl.semaphore_signal(barrier, inc=1, device_id=along(step), device_id_type=MESH)

    dims_copy.wait()
    size_c = dims_ref[0, z]
    size_d = dims_ref[1, z]
    amp_copy.wait()
    lane = lax.broadcasted_iota(jnp.int32, (ROWS, 2 * HALF), 1)
    valid = (lane // BS < size_c) & (lax.rem(lane, BS) < size_d)
    masked = jnp.where(valid, amp_v[...].astype(jnp.float32), 0.0).astype(jnp.bfloat16)
    mine_v[STAGE * STAGES - BLOCK:, :] = jnp.zeros((BLOCK, 2 * HALF), jnp.bfloat16)
    mine_v[0:ROWS, :] = masked

    pl.semaphore_wait(barrier, len(shifts) + 5)

    pending = []

    def send(src, dst, send_sem, recv_sem, to):
        copy = pltpu.make_async_remote_copy(
            src_ref=src, dst_ref=dst, send_sem=send_sem, recv_sem=recv_sem, device_id=to, device_id_type=MESH
        )
        copy.start()
        pending.append(copy)

    def arrived(dst, send_sem, recv_sem):
        pltpu.make_async_remote_copy(
            src_ref=dst, dst_ref=dst, send_sem=send_sem, recv_sem=recv_sem,
            device_id=device(here, other), device_id_type=MESH,
        ).wait_recv()

    def block(h, place, piece):
        rows = pl.ds(pl.multiple_of(place * BLOCK, BLOCK), BLOCK)
        if piece is None:
            cols = pl.ds(pl.multiple_of(core * HALF, HALF), HALF)
        else:
            cols = pl.ds(pl.multiple_of(core * HALF + piece * QUART, QUART), QUART)
        return gat.at[h, rows, cols]

    counters = {}

    def next_of(key):
        counters[key] = counters.get(key, -1) + 1
        return counters[key]

    U_M, U_P, U2_0, U2_1 = 0, 1, 2, 3

    def slot_v(kind, origin):
        return 4 + kind * 4 + ORIGINS.index(origin)

    def push(h, place, piece, slot, to):
        ref = block(h, place, piece)
        send(ref, ref, ag_send.at[h, next_of(("ag", h))], ag_recv.at[h, slot], device(to, core))

    def got(h, place, piece, slot):
        arrived(block(h, place, piece), ag_send.at[h, 0], ag_recv.at[h, slot])

    def share(h, place):
        index = next_of(("cc", h))
        ref = block(h, place, None)
        send(ref, ref, cc_send.at[h, index], cc_recv.at[h, index], device(here, other))

    def up(h, origin, piece_place):
        push(h, piece_place, None, slot_v(0, origin), rel(0, 1))
        push(h, piece_place, None, slot_v(1, origin), rel(0, -1))

    def swap(part_of):
        rows = pl.ds(part_of * BLOCK, BLOCK)
        send(mine_v.at[rows], their_v.at[rows], sw_send.at[part_of], sw_recv.at[part_of], device(here, other))

    def swapped(part_of):
        rows = pl.ds(part_of * BLOCK, BLOCK)
        arrived(their_v.at[rows], sw_send.at[part_of], sw_recv.at[part_of])

    def assemble(h):
        pair = slice(h // 2 * BLOCK, h // 2 * BLOCK + BLOCK)
        start = h % 2 * STAGE
        mine = mine_v[pair, :].astype(jnp.float32)[start:start + STAGE]
        theirs = their_v[pair, :].astype(jnp.float32)[start:start + STAGE]
        low = jnp.where(core == 0, mine, theirs)
        high = jnp.where(core == 0, theirs, mine)
        gat[h, pl.ds(pl.multiple_of(here * BLOCK, BLOCK), BLOCK), :] = jnp.concatenate([low, high], 0).astype(jnp.bfloat16)

    def own(h):
        push(h, here, None, U_M, rel(1, 0))
        push(h, here, None, U_P, rel(-1, 0))
        if h in STRAIGHT:
            push(h, here, None, U2_0, rel(2, 0))
        up(h, 0, here)

    def first_hop(h, sign):
        place = rel(-sign, 0)
        got(h, place, None, U_M if sign > 0 else U_P)
        if h in STRAIGHT:
            pass
        elif sign > 0:
            push(h, place, 0, U2_0, rel(1, 0))
        else:
            push(h, place, 1, U2_1, rel(-1, 0))
        up(h, -sign, place)
        share(h, place)

    def second_hop(h):
        place = rel(2, 0)
        if h in STRAIGHT:
            got(h, place, None, U2_0)
        else:
            got(h, place, 0, U2_0)
            got(h, place, 1, U2_1)
        up(h, 2, place)
        share(h, place)

    def column_low(h, origin):
        low = rel(origin, -1)
        got(h, low, None, slot_v(0, origin))
        push(h, low, 0, slot_v(2, origin), rel(0, 1))
        share(h, low)

    def column_high(h, origin):
        high = rel(origin, 1)
        got(h, high, None, slot_v(1, origin))
        push(h, high, 1, slot_v(3, origin), rel(0, -1))
        share(h, high)

    def column_end(h, origin):
        far = rel(origin, 2)
        got(h, far, 0, slot_v(2, origin))
        got(h, far, 1, slot_v(3, origin))
        share(h, far)

    def shared(h):
        for index in range(15):
            arrived(block(h, here, None), cc_send.at[h, 0], cc_recv.at[h, index])

    def product(h, half):
        cols = slice(half * WIDE, (half + 1) * WIDE)
        part[h, :, cols] = jnp.dot(gat[h], wts[:, cols], preferred_element_type=jnp.float32)

    def chunk(h, half, dest, lb):
        rows = pl.ds(pl.multiple_of(dest * CHUNK, CHUNK), CHUNK)
        return part[h, rows, half * WIDE + lb * 128:half * WIDE + (lb + 1) * 128]

    def decode(h, way, half, t):
        codes = rbuf[h, way, half, t, 4 * CHUNK:, :].astype(jnp.int32).astype(jnp.float32)
        scales = jnp.exp2(codes * (1.0 / CODE)) * (1.0 / TOP)
        pieces = []
        for lb in range(4):
            q = rbuf[h, way, half, t, lb * CHUNK:(lb + 1) * CHUNK, :].astype(jnp.int32).astype(jnp.float32)
            pieces.append(q * scales[lb:lb + 1, :])
        return pieces

    def landed(h, way, half, t):
        arrived(rbuf.at[h, way, half, t], rs_send.at[h, way, half, 0], rs_recv.at[h, way, half, t])

    def emit(h, way, half, slot, ahead, earlier, far):
        sign = 1 if way == 0 else -1
        dest = lax.rem(z + sign * ahead + NZ, NZ)
        before = []
        for known in earlier:
            landed(h, way, half, known)
            before.append(decode(h, way, half, known))
        row = lax.broadcasted_iota(jnp.int32, (8, 128), 0)
        codes = jnp.zeros((8, 128), jnp.float32)
        for lb in range(4):
            v = chunk(h, half, dest, lb)
            for pieces in before:
                v = v + pieces[lb]
            top = jnp.maximum(jnp.max(jnp.abs(v), axis=0, keepdims=True), 1e-30)
            code = jnp.ceil(jnp.log2(top) * CODE)
            q = jnp.round(v * (jnp.exp2(code * (-1.0 / CODE)) * TOP))
            sbuf[h, way, half, slot, lb * CHUNK:(lb + 1) * CHUNK, :] = q.astype(jnp.int32).astype(jnp.int16)
            codes = jnp.where(row == lb, code, codes)
        sbuf[h, way, half, slot, 4 * CHUNK:, :] = codes.astype(jnp.int32).astype(jnp.int16)
        send(sbuf.at[h, way, half, slot], rbuf.at[h, way, half, slot], rs_send.at[h, way, half, slot],
             rs_recv.at[h, way, half, slot], along(sign * far))

    def hop(h, way, half, t):
        reach = REACH[half][way]
        if t < reach:
            emit(h, way, half, t, reach - t, [t - 1] if t > 0 else [], 1)

    def hops(h, half, t):
        if h not in FAST:
            hop(h, 0, half, t)
            hop(h, 1, half, t)
            return
        long = 0 if REACH[half][0] == 4 else 1
        if t == 0:
            emit(h, long, half, 0, 4, [], 1)
            hop(h, 1 - long, half, 0)
            emit(h, long, half, 1, 2, [], 1)
        elif t == 1:
            emit(h, long, half, 2, 3, [0], 2)
            hop(h, 1 - long, half, 1)
        elif t == 2:
            emit(h, long, half, 3, 1, [1, 2], 1)
            hop(h, 1 - long, half, 2)

    q_out = blk // 4
    out_a = dims_ref[0, q_out]
    out_b = dims_ref[1, q_out]

    def settle(h, half):
        landed(h, 0, half, REACH[half][0] - 1)
        landed(h, 1, half, REACH[half][1] - 1)
        plus = decode(h, 0, half, REACH[half][0] - 1)
        minus = decode(h, 1, half, REACH[half][1] - 1)
        for lb in range(4):
            start = half * WIDE + lb * 128
            column = lax.broadcasted_iota(jnp.int32, (CHUNK, 128), 1) + start
            a = lax.rem(blk, 4) * 16 + column // BS
            keep = (a < out_a) & (lax.rem(column, BS) < out_b)
            total = chunk(h, half, z, lb) + plus[lb] + minus[lb]
            total = jnp.where(keep, total, 0.0)
            count = min(STAGE, ROWS - h * STAGE)
            for g in range(4):
                row0 = g * ROWS + h * STAGE
                outf[row0:row0 + count, start:start + 128] = total[g * STAGE:g * STAGE + count, :]

    def cycle_left():
        cyc_copy.wait()
        lhs[...] = jnp.zeros_like(lhs)
        for cc in range(2):
            lhs[cc * 128:cc * 128 + 120, :] = cyc_v[cc]
        lhs_t[...] = lhs[...].T

    def cycle_rows(h):
        cols = pl.ds(pl.multiple_of(blk * 128, 128), 128)
        count = min(STAGE, ROWS - h * STAGE)
        rows = gat[h, :, cols].astype(jnp.float32)
        for src in range(32):
            tbl[src * ROWS + h * STAGE:src * ROWS + h * STAGE + count, :] = rows[src * STAGE:src * STAGE + count]

    def cycle_product():
        first = lax.broadcasted_iota(jnp.int32, (120, 128), 1) < 64
        rhs[...] = jnp.zeros_like(rhs)
        for pair in range(4):
            even = tbl[pl.ds(2 * pair, 120, stride=8), :]
            odd = tbl[pl.ds(2 * pair + 1, 120, stride=8), :]
            cols = slice(pair * 128, (pair + 1) * 128)
            rhs[0:120, cols] = jnp.where(first, even, pltpu.roll(odd, 64, 1)).astype(jnp.bfloat16)
            rhs[128:248, cols] = jnp.where(first, pltpu.roll(even, 64, 1), odd).astype(jnp.bfloat16)
        for n in range(2):
            cols = slice(n * 256, (n + 1) * 256)
            term = jnp.dot(lhs_t[...], rhs[:, cols], preferred_element_type=jnp.float32)
            cyc_p[:, :, :, cols] = term.reshape(16, 2, 16, 256)
        send(cyc_p.at[:, other], cyc_x, cy_send.at[0], cy_recv.at[0], device(here, other))

    def cycle_spread():
        arrived(cyc_x, cy_send.at[0], cy_recv.at[0])
        cyc_s[...] = cyc_p[:, core] + cyc_x[...]
        for index, (dx, dy) in enumerate(shifts):
            to = chip(dx, dy)
            send(cyc_s.at[to], cyc_r.at[index], cy_send.at[1 + index], cy_recv.at[1 + index], device(to, core))

    def cycle_settle():
        total = cyc_s[here]
        for index in range(len(shifts)):
            arrived(cyc_r.at[index], cy_send.at[0], cy_recv.at[1 + index])
            total = total + cyc_r[index]
        size_a = dims_ref[0, z]
        size_b = dims_ref[1, z]
        a = lax.rem(blk, 4) * 16 + lax.broadcasted_iota(jnp.int32, (16, 512), 0)
        b = lax.rem(lax.broadcasted_iota(jnp.int32, (16, 512), 1), BS)
        cycle_ref[...] = jnp.where((a < size_a) & (b < size_b), total, 0.0).astype(jnp.bfloat16)

    swap(0)
    swap(1)
    swapped(0)
    assemble(0)
    own(0)
    assemble(1)
    swapped(1)
    for h in range(2, STAGES):
        assemble(h)
    own(1)
    first_hop(0, 1)
    first_hop(0, -1)
    column_low(0, 0)
    column_high(0, 0)
    second_hop(0)
    column_low(1, 0)
    column_high(1, 0)
    first_hop(1, 1)
    first_hop(1, -1)
    column_low(0, -1)
    column_high(0, -1)
    column_low(0, 1)
    column_high(0, 1)
    column_end(0, 0)
    column_high(0, 2)
    column_low(0, 2)
    own(2)
    second_hop(1)
    column_end(1, 0)
    column_low(1, -1)
    column_high(1, -1)
    column_low(1, 1)
    column_high(1, 1)
    own(3)
    column_end(0, -1)
    column_end(0, 1)
    column_end(0, 2)
    first_hop(2, 1)
    first_hop(2, -1)
    shared(0)
    column_low(2, 0)
    column_high(2, 0)
    for copy in wts_copies:
        copy.wait()
    cycle_left()
    product(0, 0)
    hops(0, 0, 0)
    column_low(1, 2)
    column_high(1, 2)
    column_end(1, -1)
    second_hop(2)
    column_end(1, 1)
    first_hop(3, 1)
    first_hop(3, -1)
    product(0, 1)
    hops(0, 1, 0)
    column_low(2, -1)
    column_high(2, -1)
    column_low(2, 1)
    column_high(2, 1)
    column_low(3, 0)
    hops(0, 0, 1)
    column_end(2, 0)
    column_high(3, 0)
    column_end(1, 2)
    cycle_rows(0)
    second_hop(3)
    column_low(2, 2)
    column_high(2, 2)
    shared(1)
    column_low(3, -1)
    column_high(3, -1)
    product(1, 0)
    hops(0, 1, 1)
    hops(1, 0, 0)
    column_end(2, -1)
    hops(0, 0, 2)
    column_end(2, 1)
    column_low(3, 1)
    column_high(3, 1)
    column_end(3, 0)
    column_low(3, 2)
    column_end(2, 2)
    column_high(3, 2)
    product(1, 1)
    hops(1, 1, 0)
    shared(2)
    column_end(3, -1)
    product(2, 0)
    hops(0, 1, 2)
    hops(1, 0, 1)
    hops(2, 0, 0)
    column_end(3, 1)
    column_end(3, 2)
    product(2, 1)
    hops(1, 1, 1)
    hops(2, 1, 0)
    shared(3)
    product(3, 0)
    hops(3, 0, 0)
    product(3, 1)
    hops(1, 0, 2)
    hops(2, 0, 1)
    hops(3, 1, 0)
    settle(0, 0)
    settle(0, 1)
    hops(1, 1, 2)
    cycle_rows(1)
    cycle_rows(2)
    hops(2, 1, 1)
    cycle_rows(3)
    cycle_product()
    hops(3, 0, 1)
    settle(1, 0)
    hops(2, 0, 2)
    hops(3, 1, 1)
    cycle_spread()
    settle(1, 1)
    hops(2, 1, 2)
    hops(3, 0, 2)
    hops(2, 0, 3)
    hops(3, 1, 2)
    hops(2, 1, 3)
    cycle_settle()
    settle(3, 0)
    settle(2, 0)
    settle(3, 1)
    settle(2, 1)
    ladder_ref[...] = outf[...].astype(jnp.bfloat16)
    for copy in pending:
        copy.wait_send()


def local(amplitudes, ladder_ints, cycle_ints, block_dims):
    any_space = pl.BlockSpec(memory_space=pl.ANY)
    vmem = pl.BlockSpec(memory_space=pltpu.VMEM)
    dma = pltpu.SemaphoreType.DMA
    ladder, cycle = pl.pallas_call(
        kernel,
        out_shape=(
            jax.ShapeDtypeStruct((120, 1024), jnp.bfloat16),
            jax.ShapeDtypeStruct((16, 512), jnp.bfloat16),
        ),
        in_specs=[any_space, any_space, any_space, any_space],
        out_specs=(vmem, vmem),
        scratch_shapes=[
            pltpu.SMEM((2, 8), jnp.int32),
            pltpu.VMEM((ROWS, 2 * HALF), jnp.bfloat16),
            pltpu.VMEM((STAGE * STAGES, 2 * HALF), jnp.bfloat16),
            pltpu.VMEM((STAGE * STAGES, 2 * HALF), jnp.bfloat16),
            pltpu.VMEM((STAGES, 256, 4096), jnp.bfloat16),
            pltpu.VMEM((4096, 1024), jnp.bfloat16),
            pltpu.VMEM((2, 120, 512), jnp.bfloat16),
            pltpu.VMEM((STAGES, 256, 1024), jnp.float32),
            pltpu.VMEM((STAGES, 2, 2, 4, 4 * CHUNK + 8, 128), jnp.int16),
            pltpu.VMEM((STAGES, 2, 2, 4, 4 * CHUNK + 8, 128), jnp.int16),
            pltpu.VMEM((120, 1024), jnp.float32),
            pltpu.VMEM((960, 128), jnp.float32),
            pltpu.VMEM((256, 512), jnp.bfloat16),
            pltpu.VMEM((256, 512), jnp.bfloat16),
            pltpu.VMEM((512, 256), jnp.bfloat16),
            pltpu.VMEM((16, 2, 16, 512), jnp.float32),
            pltpu.VMEM((16, 16, 512), jnp.float32),
            pltpu.VMEM((16, 16, 512), jnp.float32),
            pltpu.VMEM((15, 16, 512), jnp.float32),
            dma((11,)),
            dma((2,)),
            dma((2,)),
            dma((STAGES, 20)),
            dma((STAGES, 20)),
            dma((STAGES, 15)),
            dma((STAGES, 15)),
            dma((STAGES, 2, 2, 4)),
            dma((STAGES, 2, 2, 4)),
            dma((16,)),
            dma((16,)),
        ],
        compiler_params=pltpu.CompilerParams(
            collective_id=0, has_side_effects=True, vmem_limit_bytes=56 << 20
        ),
    )(amplitudes, ladder_ints, cycle_ints[0], block_dims.T)
    def hand_over(ladder_in, cycle_in, ladder_out, cycle_out):
        ladder_out[...] = ladder_in[...]
        cycle_out[...] = cycle_in[...]

    ladder, cycle = pl.pallas_call(
        hand_over,
        out_shape=(
            jax.ShapeDtypeStruct((120, 1024), jnp.bfloat16),
            jax.ShapeDtypeStruct((16, 512), jnp.bfloat16),
        ),
        in_specs=[vmem, vmem],
        out_specs=(vmem, vmem),
    )(ladder, cycle)
    return ladder, cycle[None]


def solution(mesh):
    in_specs = (P("blk", "slab"), P("slab", "blk"), P("slab", "blk", None, None), P())
    out_specs = (P("slab", "blk"), P("slab", "blk", None))
    return jax.shard_map(local, mesh=mesh, in_specs=in_specs, out_specs=out_specs, check_vma=False)
```
